32 devices in a mesh: lat: 16 (over z, x, core), chan: 2 (over y).
Axes of the slice: x: 2, y: 2, z: 4, core: 2. Of those that a mesh axis runs over, the one named last changes fastest.
Arguments:
- ocean_state: bfloat16 [384, 256, 1440], P('lat', 'chan'), may hold values from -6 to 6
- land_mask: int32 [384, 1440], P('lat', 'chan'), may hold values 0 or 1
- order_table: int32 [384], replicated, may hold values from 0 to 383, each once
- spectral_weight: bfloat16 [384, 2, 256, 256], P('lat', None, 'chan'), may hold values from -0.25 to 0.25
- inner_weight: bfloat16 [256, 512], P(None, 'chan'), may hold values from -0.375 to 0.375
- outer_weight: bfloat16 [512, 256], P('chan'), may hold values from -0.25 to 0.25
Outputs:
- layer_output: bfloat16 [384, 1440, 256], P('lat', 'chan')
The draws below stay inside these ranges and needn't reach their ends.
Inputs may be any that keep to these rules, and one draw needn't show every extreme that they name: `order_table`: a permutation: every order from 0 to 383 stands in exactly one slot.
All inputs are finite; a program needn't handle non-finite values. Where the reference program divides by a largest or mean magnitude, that divisor is 1e-20 or more. No bound on the sum of `land_mask` on one device may be relied on, other than what follows from the above.
Results may differ from the reference program's by a relative error of at most 0.0095.
Values may be sent and summed in bfloat16 or wider, within the bound.
No kernel may reach another device: no remote copies, remote signals or barrier semaphores. Data moves between devices by JAX's collectives and lax.ppermute only.
A program may use at most 128 MiB of HBM per device.

```python
import math
import jax
import jax.numpy as jnp
from jax import lax

NLAT = 384
NLON = 1440
MODES = 384
CHANNELS = 256
FFN = 512


def plant(drawn, own_key, smallest, high):
    longest = drawn.shape.index(max(drawn.shape))
    spots = []
    for shift in (0, 1):
        where = [jax.random.randint(jax.random.fold_in(own_key, axis), (), 0, length) for axis, length in enumerate(drawn.shape)]
        where[longest] = (where[longest] + shift) % drawn.shape[longest]
        spots.append(tuple(where))
    return drawn.at[spots[0]].set(smallest).at[spots[1]].set(high)


def level_of(key, dims, shards, least, top_value):
    factor_of = 1.0
    for dim, blocks in shards:
        heights = jax.random.uniform(jax.random.fold_in(jax.random.fold_in(key, 6), dim), (blocks,), jnp.float32, least / len(shards), top_value / len(shards))
        factor_of = factor_of * jnp.repeat(jnp.exp(heights), dims[dim] // blocks).reshape((-1,) + (1,) * (len(dims) - 1 - dim))
    return factor_of


def bell_draw(rng, extent, scale, reach, split=(), kind=jnp.bfloat16):
    values = scale * jax.random.normal(rng, extent, jnp.float32)
    if split:
        values = values * level_of(rng, extent, split, -0.22, 0.18)
    return jnp.clip(values, -reach, reach).astype(kind)


def setup_inputs(seed: int = 0) -> dict:
    splits = jax.random.split(jax.random.key(seed), 7)
    ocean_state = bell_draw(splits[0], (NLAT, CHANNELS, NLON), 1.0, 6.0, ((0, 16), (1, 2)))
    land_mask = plant((jax.random.randint(splits[1], (NLAT, NLON), 0, 10) < 7).astype(jnp.int32), jax.random.fold_in(splits[1], 1), 0, 1)
    order_table = jax.random.permutation(splits[2], MODES).astype(jnp.int32)
    spectral_weight = bell_draw(splits[3], (MODES, 2, CHANNELS, CHANNELS), (2 * CHANNELS) ** -0.5, 0.25, ((0, 16), (2, 2)))
    inner_weight = bell_draw(splits[4], (CHANNELS, FFN), CHANNELS ** -0.5, 0.375, ((1, 2),))
    outer_weight = bell_draw(splits[5], (FFN, CHANNELS), FFN ** -0.5, 0.25, ((0, 2),))
    return {"ocean_state": ocean_state, "land_mask": land_mask, "order_table": order_table, "spectral_weight": spectral_weight, "inner_weight": inner_weight, "outer_weight": outer_weight}


def fejer_weights():
    colatitude = (jnp.arange(NLAT, dtype=jnp.float32) + 0.5) * (math.pi / NLAT)
    harmonic = jnp.arange(1, NLAT // 2 + 1).astype(jnp.float32)
    series = jnp.cos(2.0 * colatitude[:, None] * harmonic[None, :]) / (4.0 * harmonic * harmonic - 1.0)[None, :]
    return 2.0 / NLAT * (1.0 - 2.0 * lax.optimization_barrier(jnp.sum(series, axis=1)))

def compose(earlier, latter):
    first_mat, first_log = earlier
    second_mat, second_log = latter
    product = jnp.stack([second_mat[0] * first_mat[0] + second_mat[1] * first_mat[2], second_mat[0] * first_mat[1] + second_mat[1] * first_mat[3], second_mat[2] * first_mat[0] + second_mat[3] * first_mat[2], second_mat[2] * first_mat[1] + second_mat[3] * first_mat[3]])
    largest = lax.optimization_barrier(jnp.max(jnp.abs(product), axis=0, keepdims=True))
    return (product / largest, first_log + second_log + jnp.log(largest))

def legendre_rows(order_value):
    half_rows = NLAT // 2
    colatitude = (jnp.arange(half_rows, dtype=jnp.float32) + 0.5) * (math.pi / NLAT)
    cosine = jnp.cos(colatitude)
    sine_part = jnp.sin(colatitude)
    offsets = jnp.arange(MODES).astype(jnp.float32)
    order_float = order_value.astype(jnp.float32)
    degree = order_float + offsets
    beyond_start = offsets >= 1.0
    denominator = jnp.where(beyond_start, degree * degree - order_float * order_float, 1.0)
    upper_coef = jnp.sqrt((4.0 * degree * degree - 1.0) / denominator)
    previous = degree - 1.0
    lower_coef = jnp.sqrt(jnp.maximum(previous * previous - order_float * order_float, 0.0) / jnp.maximum(4.0 * previous * previous - 1.0, 1.0))
    filled = jnp.ones((MODES, half_rows), jnp.float32)
    beyond_column = beyond_start[:, None]
    matrix = jnp.stack([jnp.where(beyond_column, upper_coef[:, None] * cosine[None, :], filled), jnp.where(beyond_column, -(upper_coef * lower_coef)[:, None] * filled, 0.0 * filled), jnp.where(beyond_column, filled, 0.0 * filled), jnp.where(beyond_column, 0.0 * filled, filled)])
    log_scale = jnp.zeros((1, MODES, half_rows), jnp.float32)
    matrix, log_scale = lax.associative_scan(compose, (matrix, log_scale), axis=1)
    steps_log = 0.5 * jnp.log((2.0 * offsets + 3.0) / (2.0 * offsets + 2.0))
    cumulative = jnp.cumsum(steps_log) - steps_log
    picked = jnp.sum(jnp.where(jnp.arange(MODES) == order_value, cumulative, 0.0 * cumulative))
    start_log = 0.5 * math.log(0.5) + picked + order_float * jnp.log(sine_part)
    northern = jnp.exp(start_log[None, :] + log_scale[0]) * matrix[0]
    northern = jnp.where((offsets < MODES - order_float)[:, None], northern, 0.0 * filled)
    parity = jnp.where(jnp.arange(MODES) % 2 == 0, 1.0, -1.0).astype(jnp.float32)
    return jnp.concatenate([northern, northern[:, ::-1] * parity[:, None]], axis=1)

def fourier_tables(orders):
    longitude = jnp.arange(NLON).astype(jnp.int32)
    phase_index = orders[:, None] * longitude[None, :] % NLON
    angles = phase_index.astype(jnp.float32) * (2.0 * math.pi / NLON)
    cosine = jnp.cos(angles)
    sine_part = jnp.sin(angles)
    forward = (jnp.concatenate([cosine, -sine_part], axis=0) * (math.sqrt(2.0 * math.pi) / NLON)).astype(jnp.bfloat16)
    factor = jnp.where(orders == 0, 1.0, 2.0).astype(jnp.float32) / math.sqrt(2.0 * math.pi)
    inverse = jnp.concatenate([cosine * factor[:, None], -sine_part * factor[:, None]], axis=0).astype(jnp.bfloat16)
    return (forward, inverse)

def mixing_blocks(weights):
    real_part = weights[:, 0]
    imag_part = weights[:, 1]
    return jnp.stack([jnp.stack([real_part, imag_part], axis=1), jnp.stack([-imag_part, real_part], axis=1)], axis=1)

def reference(ocean_state, land_mask, order_table, spectral_weight, inner_weight, outer_weight):
    forward, inverse = fourier_tables(order_table)
    flat_state = ocean_state.reshape(NLAT * CHANNELS, NLON)
    coeffs = lax.dot_general(flat_state, forward, (((1,), (1,)), ((), ())), preferred_element_type=jnp.float32)
    coeffs = coeffs.astype(jnp.bfloat16).reshape(NLAT, CHANNELS, 2, MODES)
    per_order = jnp.transpose(coeffs, (3, 0, 1, 2))
    quad_weights = fejer_weights()

    def one_order(inputs):
        order_value, row_coeffs, weight = inputs
        legendre = legendre_rows(order_value)
        weighted = (legendre * quad_weights[None, :]).astype(jnp.bfloat16)
        plain_table = legendre.astype(jnp.bfloat16)
        spectra = jnp.einsum('rcp,kr->pck', row_coeffs.astype(jnp.float32), weighted.astype(jnp.float32)).astype(jnp.bfloat16)
        blocks = mixing_blocks(weight[None])[0]
        mixed_spec = jnp.einsum('pck,pqdc->qdk', spectra.astype(jnp.float32), blocks.astype(jnp.float32)).astype(jnp.bfloat16)
        return jnp.einsum('qdk,kr->rdq', mixed_spec.astype(jnp.float32), plain_table.astype(jnp.float32)).astype(jnp.bfloat16)
    synthesis = lax.map(one_order, (order_table, per_order, spectral_weight))
    synthesis = jnp.transpose(synthesis, (1, 2, 3, 0)).reshape(NLAT * CHANNELS, 2 * MODES)
    spatial = jnp.dot(synthesis, inverse, preferred_element_type=jnp.float32).reshape(NLAT, CHANNELS, NLON)
    hidden = (ocean_state.astype(jnp.float32) + spatial).astype(jnp.bfloat16)
    ocean_mask = land_mask.astype(jnp.float32)

    def one_row(inputs):
        row_hidden, row_mask = inputs
        pre_act = lax.dot_general(row_hidden, inner_weight, (((0,), (0,)), ((), ())), preferred_element_type=jnp.float32)
        activated = jax.nn.gelu(pre_act).astype(jnp.bfloat16)
        update = jnp.dot(activated, outer_weight, preferred_element_type=jnp.float32)
        return (row_mask[:, None] * (jnp.transpose(row_hidden).astype(jnp.float32) + update)).astype(jnp.bfloat16)
    return lax.map(one_row, (hidden, ocean_mask))
```

```python
import math

import jax
import jax.numpy as jnp
from jax import lax
from jax.experimental import pallas as pl
from jax.experimental.pallas import tpu as pltpu
from jax.sharding import PartitionSpec as P

BF16 = jnp.bfloat16
F32 = jnp.float32
STEP_BITS = 64.0
BIG = 2.0**64
SMALL = 2.0**-64


def fejer_weights(nlat):
    colatitude = (jnp.arange(nlat, dtype=F32) + 0.5) * (math.pi / nlat)
    harmonic = jnp.arange(1, nlat // 2 + 1).astype(F32)
    series = (
        jnp.cos(2.0 * colatitude[:, None] * harmonic[None, :])
        / (4.0 * harmonic * harmonic - 1.0)[None, :]
    )
    return 2.0 / nlat * (1.0 - 2.0 * jnp.sum(series, axis=1))


def legendre_kernel(upper_ref, lower_ref, mant_ref, expo_ref, cos_ref, quad_ref, weighted_ref, *rest):
    plain_refs, rows_ref = rest[:-1], rest[-1]
    width = plain_refs[0].shape[2]
    modes = upper_ref.shape[1]
    nlat = cos_ref.shape[1]
    cosine = jnp.broadcast_to(cos_ref[...], (8, nlat))

    def scales(expo):
        one = jnp.ones_like(expo)
        first = jnp.where(expo < -0.5, one * SMALL, one)
        second = jnp.where(expo < -1.5, one * SMALL, one)
        return first, jnp.where(expo < -2.5, 0.0 * one, second)

    def lane_block(block, carry):
        upper = upper_ref[:, block * 128 : block * 128 + 128]
        lower = lower_ref[:, block * 128 : block * 128 + 128]

        def eight(turn, carry):
            before, last, expo, first, second, upper, lower = carry
            base = pl.multiple_of((block * 128 + turn * 8) * 8, 64)
            for j in range(8):
                a = jnp.broadcast_to(upper[:, j : j + 1], (8, nlat))
                b = jnp.broadcast_to(lower[:, j : j + 1], (8, nlat))
                fresh = (a * cosine) * last - b * before
                before, last = last, fresh
                value = (fresh * first) * second
                for c in range(nlat // 128):
                    rows_ref[c, pl.ds(base + 8 * j, 8), :] = value[:, c * 128 : c * 128 + 128]
            large = jnp.abs(last) > BIG
            before = jnp.where(large, before * SMALL, before)
            last = jnp.where(large, last * SMALL, last)
            expo = jnp.where(large, expo + 1.0, expo)
            first, second = scales(expo)
            upper = pltpu.roll(upper, 120, 1)
            lower = pltpu.roll(lower, 120, 1)
            return before, last, expo, first, second, upper, lower

        out = lax.fori_loop(0, 16, eight, carry + (upper, lower))
        return out[:5]

    expo = expo_ref[...]
    carry = (-mant_ref[...], jnp.zeros((8, nlat), F32), expo) + scales(expo)
    for block in range(modes // 128):
        carry = lane_block(block, carry)
    for c in range(nlat // 128):
        lanes = slice(c * 128, c * 128 + 128)
        quad = quad_ref[:, lanes]
        for k in range(8):
            values = rows_ref[c, pl.ds(k, modes, stride=8), :]
            at = c * 128 % width
            plain_refs[c * 128 // width][k, :, at : at + 128] = values.astype(BF16)
            weighted_ref[k, :, lanes] = (values * quad).astype(BF16)


def row_order(lat, rows, row_step):
    row = jnp.arange(lat * rows, dtype=jnp.int32)
    block, owner, inner = row // (lat * row_step), row // row_step % lat, row % row_step
    return owner * rows + block * row_step + inner


def legendre_tables(orders, row_index, quad, nlat, modes, width):
    slots = orders.shape[0]
    padded = -(-slots // 8) * 8
    orders = jnp.pad(orders, (0, padded - slots))
    half_sign = jnp.where(row_index < nlat // 2, 1.0, -1.0).astype(F32)
    theta = (jnp.minimum(row_index, nlat - 1 - row_index).astype(F32) + 0.5) * (math.pi / nlat)
    cosine = jnp.cos(theta) * half_sign
    order = orders.astype(F32)[:, None]
    offset = jnp.arange(modes).astype(F32)[None, :]
    degree = order + offset
    inside = (offset >= 1.0) & (offset < modes - order)
    upper = jnp.sqrt(
        (4.0 * degree * degree - 1.0)
        / jnp.where(offset >= 1.0, offset * (degree + order), 1.0)
    )
    previous = degree - 1.0
    lower = jnp.sqrt(
        jnp.maximum((offset - 1.0) * (previous + order), 0.0)
        / jnp.maximum(4.0 * previous * previous - 1.0, 1.0)
    )
    upper_coef = jnp.where(inside, upper, 0.0)
    lower_coef = jnp.where(inside, upper * lower, jnp.where(offset < 0.5, 1.0, 0.0))
    steps_log = 0.5 * jnp.log((2.0 * offset + 3.0) / (2.0 * offset + 2.0))
    picked = jnp.sum(jnp.where(offset < order, steps_log, 0.0), axis=1, keepdims=True)
    start_log = 0.5 * math.log(0.5) + picked + order * jnp.log(jnp.sin(theta))[None, :]
    unit = STEP_BITS * math.log(2.0)
    expo = jnp.floor(start_log / unit)
    mant = jnp.exp(start_log - expo * unit)
    eight = lambda wide: pl.BlockSpec((8, wide), lambda g: (g, 0))
    whole = lambda wide: pl.BlockSpec((1, wide), lambda g: (0, 0))
    table = lambda wide: pl.BlockSpec((8, modes, wide), lambda g: (g, 0, 0))
    shape = lambda wide: jax.ShapeDtypeStruct((padded, modes, wide), BF16)
    blocks = nlat // width
    weighted, *plain = pl.pallas_call(
        legendre_kernel,
        grid=(padded // 8,),
        in_specs=[eight(modes), eight(modes), eight(nlat), eight(nlat), whole(nlat), whole(nlat)],
        out_specs=[table(nlat)] + [table(width)] * blocks,
        out_shape=[shape(nlat)] + [shape(width)] * blocks,
        scratch_shapes=[pltpu.VMEM((nlat // 128, modes * 8, 128), F32)],
        cost_estimate=pl.CostEstimate(
            flops=padded * modes * nlat * 16, bytes_accessed=padded * modes * nlat * 4, transcendentals=0
        ),
        name="legendre",
    )(upper_coef, lower_coef, mant, expo, cosine[None, :], quad[None, :])
    return weighted[:slots], [table[:slots] for table in plain]


def fourier_columns(orders, nlon):
    inner = 8 if nlon % 8 == 0 else 1
    slots = orders.shape[0]
    column_order = jnp.repeat(orders, 2)
    part = jnp.tile(jnp.arange(2, dtype=jnp.int32), slots)
    turn = 2.0 * math.pi / nlon

    def pair(steps, shifted):
        phase = (column_order[None, :] * steps[:, None]) % nlon
        angle = phase.astype(F32) * turn
        cosine, sine = jnp.cos(angle), jnp.sin(angle)
        if not shifted:
            return cosine, sine
        odd = (part == 1)[None, :]
        return jnp.where(odd, -sine, cosine), jnp.where(odd, cosine, sine)

    far_cos, far_sin = pair(jnp.arange(nlon // inner, dtype=jnp.int32) * inner, True)
    near_cos, near_sin = pair(jnp.arange(inner, dtype=jnp.int32), False)
    value = far_cos[:, None, :] * near_cos[None] - far_sin[:, None, :] * near_sin[None]
    value = value.reshape(nlon, 2 * slots)
    factor = jnp.where(column_order == 0, 1.0, 2.0).astype(F32) / math.sqrt(2.0 * math.pi)
    forward = (value * (math.sqrt(2.0 * math.pi) / nlon)).astype(BF16)
    inverse = (value * factor[None, :]).astype(BF16)
    return forward, inverse


def mixing_blocks(weights):
    real_part = weights[:, 0]
    imag_part = weights[:, 1]
    return jnp.stack(
        [jnp.stack([real_part, imag_part], axis=1), jnp.stack([-imag_part, real_part], axis=1)],
        axis=1,
    )


def mlp_kernel(chan, here_ref, mask_ref, inner_ref, outer_ref, *rest):
    block_refs, out_ref = rest[:chan], rest[-1]
    channels = block_refs[0].shape[2]
    row = pl.program_id(0)
    lane = lax.broadcasted_iota(jnp.int32, mask_ref.shape, 1)
    mask = jnp.sum(jnp.where(lane == row, mask_ref[...], 0.0), axis=1, keepdims=True)
    points = jnp.concatenate([ref[0] for ref in block_refs], axis=1)
    pre_act = jnp.dot(points, inner_ref[...], preferred_element_type=F32)
    activated = jax.nn.gelu(pre_act).astype(BF16)
    update = jnp.dot(activated, outer_ref[...], preferred_element_type=F32)
    for shift, block_ref in enumerate(block_refs):
        start = pl.multiple_of(lax.rem(here_ref[0] - shift + chan, chan) * channels, channels)
        lanes = slice(shift * channels, (shift + 1) * channels)
        total = mask * (block_ref[0].astype(F32) + update[:, lanes])
        out_ref[0, :, pl.ds(start, channels)] = total.astype(BF16)


def mlp_rows(chan, here, blocks, mask, inner, outer, filled, row, rows, kept_at):
    row_step = mask.shape[0]
    _, piece, channels = blocks[0].shape
    whole = lambda shape: pl.BlockSpec(shape, lambda r, h: (0, 0))
    in_specs = [whole((piece, row_step)), whole(inner.shape), whole(outer.shape)]
    in_specs += [pl.BlockSpec((1, piece, channels), lambda r, h: (r + kept_at, 0, 0))]
    in_specs += [pl.BlockSpec((1, piece, channels), lambda r, h: (r, 0, 0))] * (chan - 1)
    operands = [here.reshape(1), mask.T, inner, outer] + blocks
    aliases = {}
    if filled is not None:
        aliases = {len(operands): 0}
        operands.append(filled)
        in_specs.append(pl.BlockSpec(memory_space=pl.ANY))
    width = chan * channels
    return pl.pallas_call(
        lambda *refs: mlp_kernel(chan, *refs),
        grid_spec=pltpu.PrefetchScalarGridSpec(
            num_scalar_prefetch=1,
            grid=(row_step,),
            in_specs=in_specs,
            out_specs=pl.BlockSpec((1, piece, width), lambda r, h: (r + row, 0, 0)),
        ),
        out_shape=jax.ShapeDtypeStruct((rows, piece, width), BF16),
        input_output_aliases=aliases,
        cost_estimate=pl.CostEstimate(
            flops=4 * row_step * piece * width * inner.shape[1],
            bytes_accessed=4 * row_step * piece * width,
            transcendentals=row_step * piece * inner.shape[1],
        ),
        name="pointwise",
    )(*operands)


def local(lat, chan, ocean_state, land_mask, order_table, spectral_weight, inner_weight, outer_weight):
    rows, channels, nlon = ocean_state.shape
    slots = spectral_weight.shape[0]
    modes = order_table.shape[0]
    nlat = rows * lat
    piece = nlon // chan
    slot_step = 8 if slots % 8 == 0 else slots
    row_step = 8 if rows % 8 == 0 and lat * 8 % 128 == 0 else rows
    width = lat * row_step
    here = lax.axis_index("chan")

    def ring(value, shift):
        return lax.ppermute(value, "chan", [(i, (i + shift) % chan) for i in range(chan)])

    def swap(value):
        return lax.all_to_all(value, "lat", split_axis=0, concat_axis=0, tiled=True)

    inner_full = jnp.concatenate(
        [inner_weight] + [ring(inner_weight, shift) for shift in range(1, chan)], axis=1
    )
    outer_full = jnp.concatenate(
        [outer_weight] + [ring(outer_weight, shift) for shift in range(1, chan)], axis=0
    )
    pieces = [(here + shift) % chan for shift in range(chan)]
    sources = [(here - shift) % chan for shift in range(chan)]
    take = lambda value, at, size, axis: lax.dynamic_slice_in_dim(value, at * size, size, axis=axis)
    ring_inner = jnp.concatenate([take(inner_full, at, channels, 0) for at in sources], axis=0)
    ring_outer = jnp.concatenate([take(outer_full, at, channels, 1) for at in sources], axis=1)
    my_orders = lax.dynamic_slice_in_dim(order_table, lax.axis_index("lat") * slots, slots)
    by_owner = order_table.reshape(lat, slots)
    starts = range(0, slots, slot_step)
    received, inverses = [], []
    for start in starts:
        orders = by_owner[:, start : start + slot_step].reshape(-1)
        forward, inverse = fourier_columns(orders, nlon)
        inverses.append(inverse)
        coeffs = lax.dot_general(
            forward, ocean_state, (((0,), (2,)), ((), ())), preferred_element_type=F32
        ).astype(BF16)
        received.append(swap(coeffs))
    mixers = lax.optimization_barrier(
        [
            [
                mixing_blocks(take(spectral_weight[start : start + slot_step], at, channels, 3))
                for at in sources
            ]
            for start in starts
        ]
    )
    row_index = row_order(lat, rows, row_step)
    quad = fejer_weights(nlat)[row_index]
    mixed, plains = [], []
    for index, (coeffs, start) in enumerate(zip(received, starts)):
        weighted, plain = legendre_tables(
            my_orders[start : start + slot_step], row_index, quad, nlat, modes, width
        )
        plains.append(plain)
        coeffs = coeffs.reshape(lat, slot_step, 2, rows // row_step, row_step, channels)
        coeffs = jnp.transpose(coeffs, (1, 2, 3, 0, 4, 5)).reshape(slot_step, 2, nlat, channels)
        spectra = jnp.einsum(
            "sprc,sir->spic", coeffs, weighted, preferred_element_type=F32
        ).astype(BF16)
        total = None
        for shift in range(chan):
            arrived = spectra if shift == 0 else ring(spectra, shift)
            term = jnp.einsum("spic,spqdc->sqid", arrived, mixers[index][shift], preferred_element_type=F32)
            if shift == 0 and chan > 1:
                term = lax.optimization_barrier(term)
            total = term if total is None else total + term
        mixed.append(total.astype(BF16))
    inverse = jnp.concatenate(inverses, axis=1)
    inverse_of = lax.optimization_barrier(
        [lax.dynamic_slice_in_dim(inverse, at * piece, piece) for at in pieces]
    )
    state = jnp.transpose(ocean_state.reshape(rows, channels, chan, piece), (2, 0, 3, 1))
    state = [
        lax.dynamic_index_in_dim(state, at, 0, keepdims=False) for at in pieces
    ]
    states = lax.optimization_barrier(
        [[value[row : row + row_step] for value in state] for row in range(0, rows, row_step)]
    )
    out, outs = None, []
    count = len(starts)
    for block, row in enumerate(range(0, rows, row_step)):
        back = []
        groups = [list(range(count))]
        if block == 0 and count > 1:
            groups = [list(range(count - 1)), [count - 1]]
        if block == 1 and count > 2:
            groups = [[0], list(range(1, count))]
        for group in groups:
            sent = [
                jnp.einsum("sqid,sir->rsqd", mixed[g], plains[g][block], preferred_element_type=F32)
                .astype(BF16)
                .reshape(lat, row_step, slot_step, 2, channels)
                for g in group
            ]
            sent = jnp.stack(sent, axis=1)
            arrived = swap(sent)
            back.append(jnp.transpose(arrived, (2, 1, 0, 3, 4, 5)).reshape(row_step, -1, channels))
        back = jnp.concatenate(back, axis=1)

        def points(shift):
            spatial = jnp.einsum("rkd,jk->rjd", back, inverse_of[shift], preferred_element_type=F32)
            return (states[block][shift].astype(F32) + spatial).astype(BF16)

        fast = channels % 128 == 0 and piece % 8 == 0
        parts = 2 if fast and row + row_step == rows and row_step % 8 == 0 else 1
        part_rows = row_step // parts
        blocks = [[] for _ in range(parts)]
        for shift in range(1, chan):
            leaving = points(shift)
            for part in range(parts):
                blocks[part].append(ring(leaving[part * part_rows : (part + 1) * part_rows], shift))
        kept = points(0)
        ocean_mask = land_mask[row : row + row_step].astype(F32)
        if fast:
            for part in range(parts):
                at = part * part_rows
                out = mlp_rows(
                    chan,
                    here,
                    [kept] + blocks[part],
                    ocean_mask[at : at + part_rows],
                    ring_inner,
                    ring_outer,
                    out,
                    row + at,
                    rows,
                    at,
                )
            continue
        blocks = [kept] + blocks[0]
        full = jnp.take(jnp.stack(blocks, axis=2), (here - jnp.arange(chan)) % chan, axis=2)
        full = full.reshape(row_step, piece, chan * channels)
        pre_act = jnp.einsum("rpc,ch->rph", full, inner_full, preferred_element_type=F32)
        activated = jax.nn.gelu(pre_act).astype(BF16)
        update = jnp.einsum("rph,hc->rpc", activated, outer_full, preferred_element_type=F32)
        outs.append((ocean_mask[:, :, None] * (full.astype(F32) + update)).astype(BF16))
    return jnp.concatenate(outs, axis=0) if outs else out


def solution(mesh):
    placed = (
        P("lat", "chan", None),
        P("lat", "chan"),
        P(),
        P("lat", None, "chan", None),
        P(None, "chan"),
        P("chan", None),
    )
    lat, chan = mesh.shape["lat"], mesh.shape["chan"]

    def body(*args):
        return local(lat, chan, *args)

    return jax.shard_map(
        body, mesh=mesh, in_specs=placed, out_specs=P("lat", "chan", None), check_vma=False
    )
```

```python
import math

import jax
import jax.numpy as jnp
from jax import lax
from jax.experimental import pallas as pl
from jax.experimental.pallas import tpu as pltpu
from jax.sharding import PartitionSpec as P

BF16 = jnp.bfloat16
F32 = jnp.float32
STEP_BITS = 64.0
BIG = 2.0**64
SMALL = 2.0**-64


def turn_pair(count, period):
    count = count.astype(F32)
    count = count - jnp.floor(count * (1.0 / period)) * period
    quarter = jnp.floor(count * (4.0 / period) + 0.5)
    angle = (4.0 * count - quarter * period) * (math.pi / (2.0 * period))
    square = angle * angle
    cosine, sine = 1.0 / math.factorial(10), 1.0 / math.factorial(11)
    for k in (4, 3, 2, 1, 0):
        cosine = 1.0 / math.factorial(2 * k) - square * cosine
        sine = 1.0 / math.factorial(2 * k + 1) - square * sine
    sine = sine * angle
    quarter = quarter - 4.0 * jnp.floor(quarter * 0.25)
    odd = (quarter == 1.0) | (quarter == 3.0)
    first, second = jnp.where(odd, sine, cosine), jnp.where(odd, cosine, sine)
    first = jnp.where((quarter == 1.0) | (quarter == 2.0), -first, first)
    return first, jnp.where(quarter >= 2.0, -second, second)


def fejer_weights(row_index, nlat):
    harmonic = jnp.arange(1, nlat // 2 + 1, dtype=jnp.int32)
    cosine, _ = turn_pair(harmonic[:, None] * (2 * row_index + 1)[None, :], 2 * nlat)
    harmonic = harmonic.astype(F32)
    series = cosine / (4.0 * harmonic * harmonic - 1.0)[:, None]
    return 2.0 / nlat * (1.0 - 2.0 * jnp.sum(series, axis=0))


def legendre_kernel(upper_ref, lower_ref, mant_ref, expo_ref, cos_ref, quad_ref, weighted_ref, *rest):
    plain_refs, rows_ref = rest[:-1], rest[-1]
    width = plain_refs[0].shape[2]
    slots, modes = upper_ref.shape
    nlat = cos_ref.shape[1]
    groups = range(slots // 8)

    def scales(expo):
        one = jnp.ones_like(expo)
        first = jnp.where(expo < -0.5, one * SMALL, one)
        second = jnp.where(expo < -1.5, one * SMALL, one)
        return first, jnp.where(expo < -2.5, 0.0 * one, second)

    @pl.when(pl.program_id(0) == 0)
    def _():
        cosine = jnp.broadcast_to(cos_ref[...], (8, nlat))

        def eight(lane, carry):
            states, coefs = carry
            base = lane * (8 * slots)
            states = list(states)
            for j in range(8):
                for g in groups:
                    before, last, expo, first, second = states[g]
                    upper, lower = coefs[g]
                    a = jnp.broadcast_to(upper[:, j : j + 1], (8, nlat))
                    b = jnp.broadcast_to(lower[:, j : j + 1], (8, nlat))
                    fresh = (a * cosine) * last - b * before
                    states[g] = (last, fresh, expo, first, second)
                    value = (fresh * first) * second
                    at = pl.multiple_of(base + j * slots + 8 * g, 8)
                    for c in range(nlat // 128):
                        rows_ref[c, pl.ds(at, 8), :] = value[:, c * 128 : c * 128 + 128]
            for g in groups:
                before, last, expo, first, second = states[g]
                large = jnp.abs(last) > BIG
                before = jnp.where(large, before * SMALL, before)
                last = jnp.where(large, last * SMALL, last)
                expo = jnp.where(large, expo + 1.0, expo)
                states[g] = (before, last, expo) + scales(expo)
            coefs = tuple((pltpu.roll(u, 120, 1), pltpu.roll(w, 120, 1)) for u, w in coefs)
            return tuple(states), coefs

        states = []
        for g in groups:
            expo = expo_ref[8 * g : 8 * g + 8, :]
            mant = mant_ref[8 * g : 8 * g + 8, :]
            states.append((-mant, jnp.zeros((8, nlat), F32), expo) + scales(expo))
        states = tuple(states)

        def lane_block(block, states):
            lanes = pl.ds(pl.multiple_of(block * 128, 128), 128)
            coefs = tuple(
                (upper_ref[8 * g : 8 * g + 8, lanes], lower_ref[8 * g : 8 * g + 8, lanes]) for g in groups
            )
            body = lambda turn, carry: eight(block * 16 + turn, carry)
            return lax.fori_loop(0, 16, body, (states, coefs))[0]

        lax.fori_loop(0, modes // 128, lane_block, states)

    for c in range(nlat // 128):
        lanes = slice(c * 128, c * 128 + 128)
        quad = quad_ref[:, lanes]
        plain_ref, at = plain_refs[c * 128 // width], c * 128 % width

        @pl.loop(0, 8)
        def _(k):
            values = rows_ref[c, pl.ds(pl.program_id(0) * 8 + k, modes, stride=slots), :]
            plain_ref[k, :, at : at + 128] = values.astype(BF16)
            weighted_ref[k, :, lanes] = (values * quad).astype(BF16)


def row_order(lat, rows, row_step):
    row = jnp.arange(lat * rows, dtype=jnp.int32)
    block, owner, inner = row // (lat * row_step), row // row_step % lat, row % row_step
    return owner * rows + block * row_step + inner


def legendre_tables(orders, row_index, quad, nlat, modes, width):
    slots = orders.shape[0]
    padded = -(-slots // 8) * 8
    orders = jnp.pad(orders, (0, padded - slots))
    half_sign = jnp.where(row_index < nlat // 2, 1.0, -1.0).astype(F32)
    north = jnp.minimum(row_index, nlat - 1 - row_index)
    cosine, sine = turn_pair(2 * north + 1, 4 * nlat)
    cosine = cosine * half_sign
    order = orders.astype(F32)[:, None]
    offset = jnp.arange(modes).astype(F32)[None, :]
    degree = order + offset
    inside = (offset >= 1.0) & (offset < modes - order)
    upper = jnp.sqrt(
        (4.0 * degree * degree - 1.0)
        / jnp.where(offset >= 1.0, offset * (degree + order), 1.0)
    )
    previous = degree - 1.0
    lower = jnp.sqrt(
        jnp.maximum((offset - 1.0) * (previous + order), 0.0)
        / jnp.maximum(4.0 * previous * previous - 1.0, 1.0)
    )
    upper_coef = jnp.where(inside, upper, 0.0)
    lower_coef = jnp.where(inside, upper * lower, jnp.where(offset < 0.5, 1.0, 0.0))
    steps_log = 0.5 * jnp.log((2.0 * offset + 3.0) / (2.0 * offset + 2.0))
    picked = jnp.sum(jnp.where(offset < order, steps_log, 0.0), axis=1, keepdims=True)
    start_log = 0.5 * math.log(0.5) + picked + order * jnp.log(sine)[None, :]
    unit = STEP_BITS * math.log(2.0)
    expo = jnp.floor(start_log / unit)
    mant = jnp.exp(start_log - expo * unit)
    each = lambda wide: pl.BlockSpec((padded, wide), lambda g: (0, 0))
    whole = lambda wide: pl.BlockSpec((1, wide), lambda g: (0, 0))
    table = lambda wide: pl.BlockSpec((8, modes, wide), lambda g: (g, 0, 0))
    shape = lambda wide: jax.ShapeDtypeStruct((padded, modes, wide), BF16)
    blocks = nlat // width
    weighted, *plain = pl.pallas_call(
        legendre_kernel,
        grid=(padded // 8,),
        in_specs=[each(modes), each(modes), each(nlat), each(nlat), whole(nlat), whole(nlat)],
        out_specs=[table(nlat)] + [table(width)] * blocks,
        out_shape=[shape(nlat)] + [shape(width)] * blocks,
        scratch_shapes=[pltpu.VMEM((nlat // 128, modes * padded, 128), F32)],
        cost_estimate=pl.CostEstimate(
            flops=padded * modes * nlat * 16, bytes_accessed=padded * modes * nlat * 4, transcendentals=0
        ),
        name="legendre",
    )(upper_coef, lower_coef, mant, expo, cosine[None, :], quad[None, :])
    return weighted[:slots], [table[:slots] for table in plain]


def fourier_columns(orders, nlon):
    inner = 8 if nlon % 8 == 0 else 1
    slots = orders.shape[0]
    column_order = jnp.repeat(orders, 2)
    part = jnp.tile(jnp.arange(2, dtype=jnp.int32), slots)

    def pair(steps, shifted):
        cosine, sine = turn_pair(column_order[None, :] * steps[:, None], nlon)
        if not shifted:
            return cosine, sine
        odd = (part == 1)[None, :]
        return jnp.where(odd, -sine, cosine), jnp.where(odd, cosine, sine)

    far_cos, far_sin = pair(jnp.arange(nlon // inner, dtype=jnp.int32) * inner, True)
    near_cos, near_sin = pair(jnp.arange(inner, dtype=jnp.int32), False)
    value = far_cos[:, None, :] * near_cos[None] - far_sin[:, None, :] * near_sin[None]
    value = value.reshape(nlon, 2 * slots)
    factor = jnp.where(column_order == 0, 1.0, 2.0).astype(F32) / math.sqrt(2.0 * math.pi)
    forward = (value * (math.sqrt(2.0 * math.pi) / nlon)).astype(BF16)
    inverse = (value * factor[None, :]).astype(BF16)
    return forward, inverse


def mixing_blocks(weights):
    real_part = weights[:, 0]
    imag_part = weights[:, 1]
    return jnp.stack(
        [jnp.stack([real_part, imag_part], axis=1), jnp.stack([-imag_part, real_part], axis=1)],
        axis=1,
    )


def mlp_kernel(chan, here_ref, mask_ref, inner_ref, outer_ref, *rest):
    block_refs, out_ref = rest[:chan], rest[-1]
    channels = block_refs[0].shape[2]
    row = pl.program_id(0)
    lane = lax.broadcasted_iota(jnp.int32, mask_ref.shape, 1)
    mask = jnp.sum(jnp.where(lane == row, mask_ref[...], 0.0), axis=1, keepdims=True)
    points = jnp.concatenate([ref[0] for ref in block_refs], axis=1)
    pre_act = jnp.dot(points, inner_ref[...], preferred_element_type=F32)
    activated = jax.nn.gelu(pre_act).astype(BF16)
    update = jnp.dot(activated, outer_ref[...], preferred_element_type=F32)
    for shift, block_ref in enumerate(block_refs):
        start = pl.multiple_of(lax.rem(here_ref[0] - shift + chan, chan) * channels, channels)
        lanes = slice(shift * channels, (shift + 1) * channels)
        total = mask * (block_ref[0].astype(F32) + update[:, lanes])
        out_ref[0, :, pl.ds(start, channels)] = total.astype(BF16)


def mlp_rows(chan, here, blocks, mask, inner, outer, filled, row, rows, kept_at):
    row_step = mask.shape[0]
    _, piece, channels = blocks[0].shape
    whole = lambda shape: pl.BlockSpec(shape, lambda r, h: (0, 0))
    in_specs = [whole((piece, row_step)), whole(inner.shape), whole(outer.shape)]
    in_specs += [pl.BlockSpec((1, piece, channels), lambda r, h: (r + kept_at, 0, 0))]
    in_specs += [pl.BlockSpec((1, piece, channels), lambda r, h: (r, 0, 0))] * (chan - 1)
    operands = [here.reshape(1), mask.T, inner, outer] + blocks
    aliases = {}
    if filled is not None:
        aliases = {len(operands): 0}
        operands.append(filled)
        in_specs.append(pl.BlockSpec(memory_space=pl.ANY))
    width = chan * channels
    return pl.pallas_call(
        lambda *refs: mlp_kernel(chan, *refs),
        grid_spec=pltpu.PrefetchScalarGridSpec(
            num_scalar_prefetch=1,
            grid=(row_step,),
            in_specs=in_specs,
            out_specs=pl.BlockSpec((1, piece, width), lambda r, h: (r + row, 0, 0)),
        ),
        out_shape=jax.ShapeDtypeStruct((rows, piece, width), BF16),
        input_output_aliases=aliases,
        cost_estimate=pl.CostEstimate(
            flops=4 * row_step * piece * width * inner.shape[1],
            bytes_accessed=4 * row_step * piece * width,
            transcendentals=row_step * piece * inner.shape[1],
        ),
        name="pointwise",
    )(*operands)


def local(lat, chan, ocean_state, land_mask, order_table, spectral_weight, inner_weight, outer_weight):
    rows, channels, nlon = ocean_state.shape
    slots = spectral_weight.shape[0]
    modes = order_table.shape[0]
    nlat = rows * lat
    piece = nlon // chan
    slot_step = 8 if slots % 8 == 0 else slots
    row_step = 8 if rows % 8 == 0 and lat * 8 % 128 == 0 else rows
    width = lat * row_step
    here = lax.axis_index("chan")

    def ring(value, shift):
        return lax.ppermute(value, "chan", [(i, (i + shift) % chan) for i in range(chan)])

    def swap(value):
        return lax.all_to_all(value, "lat", split_axis=0, concat_axis=0, tiled=True)

    inner_parts = [inner_weight] + [ring(inner_weight, shift) for shift in range(1, chan)]
    outer_parts = [outer_weight] + [ring(outer_weight, shift) for shift in range(1, chan)]
    inner_full = jnp.concatenate(inner_parts, axis=1)
    outer_full = jnp.concatenate(outer_parts, axis=0)
    pieces = [(here + shift) % chan for shift in range(chan)]
    sources = [(here - shift) % chan for shift in range(chan)]
    take = lambda value, at, size, axis: lax.dynamic_slice_in_dim(value, at * size, size, axis=axis)
    order_of = [[(at - shift) % chan for shift in range(chan)] for at in range(chan)]
    arranged = lambda value, axis, at: jnp.concatenate(
        [jnp.split(value, chan, axis=axis)[block] for block in order_of[at]], axis=axis
    )
    ring_inner, ring_outer = arranged(inner_full, 0, 0), arranged(outer_full, 1, 0)
    for at in range(1, chan):
        ring_inner = jnp.where(here == at, arranged(inner_full, 0, at), ring_inner)
        ring_outer = jnp.where(here == at, arranged(outer_full, 1, at), ring_outer)
    ring_inner, ring_outer = lax.optimization_barrier((ring_inner, ring_outer))
    my_orders = lax.dynamic_slice_in_dim(order_table, lax.axis_index("lat") * slots, slots)
    by_owner = order_table.reshape(lat, slots)
    starts = range(0, slots, slot_step)
    received, inverses = [], []
    for start in starts:
        orders = by_owner[:, start : start + slot_step].reshape(-1)
        forward, inverse = lax.optimization_barrier(fourier_columns(orders, nlon))
        inverses.append(inverse)
        coeffs = lax.dot_general(
            forward, ocean_state, (((0,), (2,)), ((), ())), preferred_element_type=F32
        ).astype(BF16)
        received.append(swap(coeffs))
    mixers = lax.optimization_barrier(
        [
            [
                mixing_blocks(take(spectral_weight[start : start + slot_step], at, channels, 3))
                for at in sources
            ]
            for start in starts
        ]
    )
    row_index = row_order(lat, rows, row_step)
    quad = fejer_weights(row_index, nlat)
    weighted_all, plain_all = legendre_tables(my_orders, row_index, quad, nlat, modes, width)
    mixed, plains = [], []
    for index, (coeffs, start) in enumerate(zip(received, starts)):
        weighted = weighted_all[start : start + slot_step]
        plains.append([table[start : start + slot_step] for table in plain_all])
        coeffs = coeffs.reshape(lat, slot_step, 2, rows // row_step, row_step, channels)
        coeffs = jnp.transpose(coeffs, (1, 2, 3, 0, 4, 5)).reshape(slot_step, 2, nlat, channels)
        spectra = jnp.einsum(
            "sprc,sir->spic", coeffs, weighted, preferred_element_type=F32
        ).astype(BF16)
        total = None
        for shift in range(chan):
            arrived = spectra if shift == 0 else ring(spectra, shift)
            term = jnp.einsum("spic,spqdc->sqid", arrived, mixers[index][shift], preferred_element_type=F32)
            if shift == 0 and chan > 1:
                term = lax.optimization_barrier(term)
            total = term if total is None else total + term
        mixed.append(total.astype(BF16))
    inverse = jnp.concatenate(inverses, axis=1)
    inverse_of = lax.optimization_barrier(
        [lax.dynamic_slice_in_dim(inverse, at * piece, piece) for at in pieces]
    )
    fast = channels % 128 == 0 and piece % 8 == 0 and row_step % 8 == 0 and len(starts) > 1
    state = jnp.transpose(ocean_state.reshape(rows, channels, chan, piece), (2, 0, 3, 1))
    state = [lax.dynamic_index_in_dim(state, at, 0, keepdims=False) for at in pieces]
    states = lax.optimization_barrier(
        [[value[row : row + row_step] for value in state] for row in range(0, rows, row_step)]
    )
    out, outs = None, []
    count = len(starts)

    def relayout(arrived):
        return jnp.transpose(arrived, (2, 1, 0, 3, 4, 5)).reshape(arrived.shape[2], -1, channels)

    def points(back, at, state):
        spatial = jnp.einsum("rkd,jk->rjd", back, inverse_of[at], preferred_element_type=F32)
        return (state.astype(F32) + spatial).astype(BF16)

    last = rows // row_step - 1
    for block, row in enumerate(range(0, rows, row_step)):
        groups = [list(range(count))]
        if fast and block == 0:
            groups = [list(range(count - 1)), [count - 1]]
        subs = [(0, row_step)]
        if fast and block == last and block > 0:
            subs = [(0, row_step // 2), (row_step // 2, row_step)]
        sent = []
        for group in groups:
            made = [
                jnp.einsum("sqid,sir->rsqd", mixed[g], plains[g][block], preferred_element_type=F32)
                .astype(BF16)
                .reshape(lat, row_step, slot_step, 2, channels)
                for g in group
            ]
            sent.append(jnp.stack(made, axis=1))
        for sub, (low, high) in enumerate(subs):
            back = []
            for part in range(len(groups)):
                back.append(relayout(swap(sent[part][:, :, low:high])))
            back = jnp.concatenate(back, axis=1)
            kept_rows = [value[low:high] for value in states[block]]
            cuts = [0, high - low]
            if fast and block == last and sub == len(subs) - 1 and high - low > 1:
                cuts = [0, (high - low) // 2, high - low]
            blocks = [[] for _ in cuts[1:]]
            for shift in range(1, chan):
                leaving = points(back, shift, kept_rows[shift])
                for part in range(len(cuts) - 1):
                    blocks[part].append(ring(leaving[cuts[part] : cuts[part + 1]], shift))
            kept = points(back, 0, kept_rows[0])
            ocean_mask = land_mask[row + low : row + high].astype(F32)
            if not fast:
                continue
            for part in range(len(cuts) - 1):
                at = cuts[part]
                out = mlp_rows(
                    chan,
                    here,
                    [kept] + blocks[part],
                    ocean_mask[at : cuts[part + 1]],
                    ring_inner,
                    ring_outer,
                    out,
                    row + low + at,
                    rows,
                    at,
                )
        if fast:
            continue
        blocks = [kept] + blocks[0]
        full = jnp.take(jnp.stack(blocks, axis=2), (here - jnp.arange(chan)) % chan, axis=2)
        full = full.reshape(row_step, piece, chan * channels)
        pre_act = jnp.einsum("rpc,ch->rph", full, inner_full, preferred_element_type=F32)
        activated = jax.nn.gelu(pre_act).astype(BF16)
        update = jnp.einsum("rph,hc->rpc", activated, outer_full, preferred_element_type=F32)
        outs.append((ocean_mask[:, :, None] * (full.astype(F32) + update)).astype(BF16))
    return jnp.concatenate(outs, axis=0) if outs else out


def solution(mesh):
    placed = (
        P("lat", "chan", None),
        P("lat", "chan"),
        P(),
        P("lat", None, "chan", None),
        P(None, "chan"),
        P("chan", None),
    )
    lat, chan = mesh.shape["lat"], mesh.shape["chan"]

    def body(*args):
        return local(lat, chan, *args)

    return jax.shard_map(
        body, mesh=mesh, in_specs=placed, out_specs=P("lat", "chan", None), check_vma=False
    )
```

```python
import math

import jax
import jax.numpy as jnp
from jax import lax
from jax.experimental import pallas as pl
from jax.experimental.pallas import tpu as pltpu
from jax.sharding import PartitionSpec as P

BF16 = jnp.bfloat16
F32 = jnp.float32
STEP_BITS = 64.0
BIG = 2.0**64
SMALL = 2.0**-64


def turn_pair(count, period):
    count = count.astype(F32)
    count = count - jnp.floor(count * (1.0 / period)) * period
    quarter = jnp.floor(count * (4.0 / period) + 0.5)
    angle = (4.0 * count - quarter * period) * (math.pi / (2.0 * period))
    square = angle * angle
    cosine, sine = 1.0 / math.factorial(10), 1.0 / math.factorial(11)
    for k in (4, 3, 2, 1, 0):
        cosine = 1.0 / math.factorial(2 * k) - square * cosine
        sine = 1.0 / math.factorial(2 * k + 1) - square * sine
    sine = sine * angle
    quarter = quarter - 4.0 * jnp.floor(quarter * 0.25)
    odd = (quarter == 1.0) | (quarter == 3.0)
    first, second = jnp.where(odd, sine, cosine), jnp.where(odd, cosine, sine)
    first = jnp.where((quarter == 1.0) | (quarter == 2.0), -first, first)
    return first, jnp.where(quarter >= 2.0, -second, second)


def fejer_weights(row_index, nlat):
    harmonic = jnp.arange(1, nlat // 2 + 1, dtype=jnp.int32)
    cosine, _ = turn_pair(harmonic[:, None] * (2 * row_index + 1)[None, :], 2 * nlat)
    harmonic = harmonic.astype(F32)
    series = cosine / (4.0 * harmonic * harmonic - 1.0)[:, None]
    return 2.0 / nlat * (1.0 - 2.0 * jnp.sum(series, axis=0))


def legendre_kernel(upper_ref, lower_ref, mant_ref, expo_ref, cos_ref, quad_ref, weighted_ref, *rest):
    plain_refs, rows_ref = rest[:-1], rest[-1]
    width = plain_refs[0].shape[2]
    slots, modes = upper_ref.shape
    nlat = cos_ref.shape[1]
    groups = range(slots // 8)

    def scales(expo):
        one = jnp.ones_like(expo)
        first = jnp.where(expo < -0.5, one * SMALL, one)
        second = jnp.where(expo < -1.5, one * SMALL, one)
        return first, jnp.where(expo < -2.5, 0.0 * one, second)

    @pl.when(pl.program_id(0) == 0)
    def _():
        cosine = jnp.broadcast_to(cos_ref[...], (8, nlat))

        def eight(lane, carry):
            states, coefs = carry
            base = lane * (8 * slots)
            states = list(states)
            for j in range(8):
                for g in groups:
                    before, last, expo, first, second = states[g]
                    upper, lower = coefs[g]
                    a = jnp.broadcast_to(upper[:, j : j + 1], (8, nlat))
                    b = jnp.broadcast_to(lower[:, j : j + 1], (8, nlat))
                    fresh = (a * cosine) * last - b * before
                    states[g] = (last, fresh, expo, first, second)
                    value = (fresh * first) * second
                    at = pl.multiple_of(base + j * slots + 8 * g, 8)
                    for c in range(nlat // 128):
                        rows_ref[c, pl.ds(at, 8), :] = value[:, c * 128 : c * 128 + 128]
            for g in groups:
                before, last, expo, first, second = states[g]
                large = jnp.abs(last) > BIG
                before = jnp.where(large, before * SMALL, before)
                last = jnp.where(large, last * SMALL, last)
                expo = jnp.where(large, expo + 1.0, expo)
                states[g] = (before, last, expo) + scales(expo)
            coefs = tuple((pltpu.roll(u, 120, 1), pltpu.roll(w, 120, 1)) for u, w in coefs)
            return tuple(states), coefs

        states = []
        for g in groups:
            expo = expo_ref[8 * g : 8 * g + 8, :]
            mant = mant_ref[8 * g : 8 * g + 8, :]
            states.append((-mant, jnp.zeros((8, nlat), F32), expo) + scales(expo))
        states = tuple(states)

        def lane_block(block, states):
            lanes = pl.ds(pl.multiple_of(block * 128, 128), 128)
            coefs = tuple(
                (upper_ref[8 * g : 8 * g + 8, lanes], lower_ref[8 * g : 8 * g + 8, lanes]) for g in groups
            )
            body = lambda turn, carry: eight(block * 16 + turn, carry)
            return lax.fori_loop(0, 16, body, (states, coefs))[0]

        lax.fori_loop(0, modes // 128, lane_block, states)

    for c in range(nlat // 128):
        lanes = slice(c * 128, c * 128 + 128)
        quad = quad_ref[:, lanes]
        plain_ref, at = plain_refs[c * 128 // width], c * 128 % width

        @pl.loop(0, 8)
        def _(k):
            values = rows_ref[c, pl.ds(pl.program_id(0) * 8 + k, modes, stride=slots), :]
            plain_ref[k, :, at : at + 128] = values.astype(BF16)
            weighted_ref[k, :, lanes] = (values * quad).astype(BF16)


def row_order(lat, rows, row_step):
    row = jnp.arange(lat * rows, dtype=jnp.int32)
    block, owner, inner = row // (lat * row_step), row // row_step % lat, row % row_step
    return owner * rows + block * row_step + inner


def legendre_tables(orders, row_index, quad, nlat, modes, width):
    slots = orders.shape[0]
    padded = -(-slots // 8) * 8
    orders = jnp.pad(orders, (0, padded - slots))
    half_sign = jnp.where(row_index < nlat // 2, 1.0, -1.0).astype(F32)
    north = jnp.minimum(row_index, nlat - 1 - row_index)
    cosine, sine = turn_pair(2 * north + 1, 4 * nlat)
    cosine = cosine * half_sign
    order = orders.astype(F32)[:, None]
    offset = jnp.arange(modes).astype(F32)[None, :]
    degree = order + offset
    inside = (offset >= 1.0) & (offset < modes - order)
    upper = jnp.sqrt(
        (4.0 * degree * degree - 1.0)
        / jnp.where(offset >= 1.0, offset * (degree + order), 1.0)
    )
    previous = degree - 1.0
    lower = jnp.sqrt(
        jnp.maximum((offset - 1.0) * (previous + order), 0.0)
        / jnp.maximum(4.0 * previous * previous - 1.0, 1.0)
    )
    upper_coef = jnp.where(inside, upper, 0.0)
    lower_coef = jnp.where(inside, upper * lower, jnp.where(offset < 0.5, 1.0, 0.0))
    steps_log = 0.5 * jnp.log((2.0 * offset + 3.0) / (2.0 * offset + 2.0))
    picked = jnp.sum(jnp.where(offset < order, steps_log, 0.0), axis=1, keepdims=True)
    start_log = 0.5 * math.log(0.5) + picked + order * jnp.log(sine)[None, :]
    unit = STEP_BITS * math.log(2.0)
    expo = jnp.floor(start_log / unit)
    mant = jnp.exp(start_log - expo * unit)
    each = lambda wide: pl.BlockSpec((padded, wide), lambda g: (0, 0))
    whole = lambda wide: pl.BlockSpec((1, wide), lambda g: (0, 0))
    table = lambda wide: pl.BlockSpec((8, modes, wide), lambda g: (g, 0, 0))
    shape = lambda wide: jax.ShapeDtypeStruct((padded, modes, wide), BF16)
    blocks = nlat // width
    weighted, *plain = pl.pallas_call(
        legendre_kernel,
        grid=(padded // 8,),
        in_specs=[each(modes), each(modes), each(nlat), each(nlat), whole(nlat), whole(nlat)],
        out_specs=[table(nlat)] + [table(width)] * blocks,
        out_shape=[shape(nlat)] + [shape(width)] * blocks,
        scratch_shapes=[pltpu.VMEM((nlat // 128, modes * padded, 128), F32)],
        cost_estimate=pl.CostEstimate(
            flops=padded * modes * nlat * 16, bytes_accessed=padded * modes * nlat * 4, transcendentals=0
        ),
        name="legendre",
    )(upper_coef, lower_coef, mant, expo, cosine[None, :], quad[None, :])
    return weighted[:slots], [table[:slots] for table in plain]


def fourier_columns(orders, nlon):
    inner = 8 if nlon % 8 == 0 else 1
    slots = orders.shape[0]
    column_order = jnp.repeat(orders, 2)
    part = jnp.tile(jnp.arange(2, dtype=jnp.int32), slots)

    def pair(steps, shifted):
        cosine, sine = turn_pair(column_order[None, :] * steps[:, None], nlon)
        if not shifted:
            return cosine, sine
        odd = (part == 1)[None, :]
        return jnp.where(odd, -sine, cosine), jnp.where(odd, cosine, sine)

    far_cos, far_sin = pair(jnp.arange(nlon // inner, dtype=jnp.int32) * inner, True)
    near_cos, near_sin = pair(jnp.arange(inner, dtype=jnp.int32), False)
    value = far_cos[:, None, :] * near_cos[None] - far_sin[:, None, :] * near_sin[None]
    value = value.reshape(nlon, 2 * slots)
    factor = jnp.where(column_order == 0, 1.0, 2.0).astype(F32) / math.sqrt(2.0 * math.pi)
    forward = (value * (math.sqrt(2.0 * math.pi) / nlon)).astype(BF16)
    inverse = (value * factor[None, :]).astype(BF16)
    return forward, inverse


def mixing_blocks(weights):
    real_part = weights[:, 0]
    imag_part = weights[:, 1]
    return jnp.stack(
        [jnp.stack([real_part, imag_part], axis=1), jnp.stack([-imag_part, real_part], axis=1)],
        axis=1,
    )


def mlp_kernel(chan, first_row, here_ref, mask_ref, inner_ref, outer_ref, *rest):
    block_refs, out_ref = rest[:chan], rest[-1]
    channels = block_refs[0].shape[2]
    row = pl.program_id(0) + first_row
    lane = lax.broadcasted_iota(jnp.int32, mask_ref.shape, 1)
    mask = jnp.sum(jnp.where(lane == row, mask_ref[...], 0.0), axis=1, keepdims=True)
    points = jnp.concatenate([ref[0] for ref in block_refs], axis=1)
    pre_act = jnp.dot(points, inner_ref[...], preferred_element_type=F32)
    activated = jax.nn.gelu(pre_act).astype(BF16)
    update = jnp.dot(activated, outer_ref[...], preferred_element_type=F32)
    for shift, block_ref in enumerate(block_refs):
        start = pl.multiple_of(lax.rem(here_ref[0] - shift + chan, chan) * channels, channels)
        lanes = slice(shift * channels, (shift + 1) * channels)
        total = mask * (block_ref[0].astype(F32) + update[:, lanes])
        out_ref[0, :, pl.ds(start, channels)] = total.astype(BF16)


def mlp_rows(chan, here, blocks, mask, inner, outer, filled, row, row_step, kept_at):
    rows = mask.shape[1]
    _, piece, channels = blocks[0].shape
    whole = lambda shape: pl.BlockSpec(shape, lambda r, h: (0, 0))
    in_specs = [whole((piece, rows)), whole(inner.shape), whole(outer.shape)]
    in_specs += [pl.BlockSpec((1, piece, channels), lambda r, h: (r + kept_at, 0, 0))]
    in_specs += [pl.BlockSpec((1, piece, channels), lambda r, h: (r, 0, 0))] * (chan - 1)
    operands = [here.reshape(1), mask, inner, outer] + blocks
    aliases = {}
    if filled is not None:
        aliases = {len(operands): 0}
        operands.append(filled)
        in_specs.append(pl.BlockSpec(memory_space=pl.ANY))
    width = chan * channels
    return pl.pallas_call(
        lambda *refs: mlp_kernel(chan, row, *refs),
        grid_spec=pltpu.PrefetchScalarGridSpec(
            num_scalar_prefetch=1,
            grid=(row_step,),
            in_specs=in_specs,
            out_specs=pl.BlockSpec((1, piece, width), lambda r, h: (r + row, 0, 0)),
        ),
        out_shape=jax.ShapeDtypeStruct((rows, piece, width), BF16),
        input_output_aliases=aliases,
        cost_estimate=pl.CostEstimate(
            flops=4 * row_step * piece * width * inner.shape[1],
            bytes_accessed=4 * row_step * piece * width,
            transcendentals=row_step * piece * inner.shape[1],
        ),
        name="pointwise",
    )(*operands)


def local(lat, chan, ocean_state, land_mask, order_table, spectral_weight, inner_weight, outer_weight):
    rows, channels, nlon = ocean_state.shape
    slots = spectral_weight.shape[0]
    modes = order_table.shape[0]
    nlat = rows * lat
    piece = nlon // chan
    slot_step = 8 if slots % 8 == 0 else slots
    row_step = 8 if rows % 8 == 0 and lat * 8 % 128 == 0 else rows
    width = lat * row_step
    here = lax.axis_index("chan")

    def ring(value, shift):
        return lax.ppermute(value, "chan", [(i, (i + shift) % chan) for i in range(chan)])

    def swap(value):
        return lax.all_to_all(value, "lat", split_axis=0, concat_axis=0, tiled=True)

    inner_parts = [inner_weight] + [ring(inner_weight, shift) for shift in range(1, chan)]
    outer_parts = [outer_weight] + [ring(outer_weight, shift) for shift in range(1, chan)]
    inner_full = jnp.concatenate(inner_parts, axis=1)
    outer_full = jnp.concatenate(outer_parts, axis=0)
    pieces = [(here + shift) % chan for shift in range(chan)]
    sources = [(here - shift) % chan for shift in range(chan)]
    take = lambda value, at, size, axis: lax.dynamic_slice_in_dim(value, at * size, size, axis=axis)
    order_of = [[(at - shift) % chan for shift in range(chan)] for at in range(chan)]
    arranged = lambda value, axis, at: jnp.concatenate(
        [jnp.split(value, chan, axis=axis)[block] for block in order_of[at]], axis=axis
    )
    ring_inner, ring_outer = arranged(inner_full, 0, 0), arranged(outer_full, 1, 0)
    for at in range(1, chan):
        ring_inner = jnp.where(here == at, arranged(inner_full, 0, at), ring_inner)
        ring_outer = jnp.where(here == at, arranged(outer_full, 1, at), ring_outer)
    ring_inner, ring_outer = lax.optimization_barrier((ring_inner, ring_outer))
    my_orders = lax.dynamic_slice_in_dim(order_table, lax.axis_index("lat") * slots, slots)
    by_owner = order_table.reshape(lat, slots)
    starts = range(0, slots, slot_step)
    received, inverses = [], []
    for start in starts:
        orders = by_owner[:, start : start + slot_step].reshape(-1)
        forward, inverse = lax.optimization_barrier(fourier_columns(orders, nlon))
        inverses.append(inverse)
        coeffs = lax.dot_general(
            forward, ocean_state, (((0,), (2,)), ((), ())), preferred_element_type=F32
        ).astype(BF16)
        received.append(swap(coeffs))
    mixers = lax.optimization_barrier(
        [
            [
                mixing_blocks(take(spectral_weight[start : start + slot_step], at, channels, 3))
                for at in sources
            ]
            for start in starts
        ]
    )
    row_index = row_order(lat, rows, row_step)
    quad = fejer_weights(row_index, nlat)
    weighted_all, plain_all = legendre_tables(my_orders, row_index, quad, nlat, modes, width)
    mixed, plains = [], []
    for index, (coeffs, start) in enumerate(zip(received, starts)):
        weighted = weighted_all[start : start + slot_step]
        plains.append([table[start : start + slot_step] for table in plain_all])
        coeffs = coeffs.reshape(lat, slot_step, 2, rows // row_step, row_step, channels)
        coeffs = jnp.transpose(coeffs, (1, 2, 3, 0, 4, 5)).reshape(slot_step, 2, nlat, channels)
        spectra = jnp.einsum(
            "sprc,sir->spic", coeffs, weighted, preferred_element_type=F32
        ).astype(BF16)
        total = None
        for shift in range(chan):
            arrived = spectra if shift == 0 else ring(spectra, shift)
            term = jnp.einsum("spic,spqdc->sqid", arrived, mixers[index][shift], preferred_element_type=F32)
            if shift == 0 and chan > 1:
                term = lax.optimization_barrier(term)
            total = term if total is None else total + term
        mixed.append(total.astype(BF16))
    inverse = jnp.concatenate(inverses, axis=1)
    inverse_of = lax.optimization_barrier(
        [lax.dynamic_slice_in_dim(inverse, at * piece, piece) for at in pieces]
    )
    fast = channels % 128 == 0 and piece % 8 == 0 and row_step % 8 == 0 and len(starts) > 1
    state = jnp.transpose(ocean_state.reshape(rows, channels, chan, piece), (2, 0, 3, 1))
    state = [lax.dynamic_index_in_dim(state, at, 0, keepdims=False) for at in pieces]
    states = lax.optimization_barrier(
        [[value[row : row + row_step] for value in state] for row in range(0, rows, row_step)]
    )
    mask_columns = lax.optimization_barrier(land_mask.astype(F32).T)
    out, outs = None, []
    count = len(starts)

    def relayout(arrived):
        return jnp.transpose(arrived, (2, 1, 0, 3, 4, 5)).reshape(arrived.shape[2], -1, channels)

    def points(back, at, state):
        spatial = jnp.einsum("rkd,jk->rjd", back, inverse_of[at], preferred_element_type=F32)
        return (state.astype(F32) + spatial).astype(BF16)

    last = rows // row_step - 1
    for block, row in enumerate(range(0, rows, row_step)):
        groups = [list(range(count))]
        if fast and block == 0:
            groups = [list(range(count - 1)), [count - 1]]
        subs = [(0, row_step)]
        if fast and block == last and block > 0:
            subs = [(0, row_step // 2), (row_step // 2, row_step)]
        sent = []
        for group in groups:
            made = [
                jnp.einsum("sqid,sir->rsqd", mixed[g], plains[g][block], preferred_element_type=F32)
                .astype(BF16)
                .reshape(lat, row_step, slot_step, 2, channels)
                for g in group
            ]
            sent.append(jnp.stack(made, axis=1))
        for sub, (low, high) in enumerate(subs):
            back = []
            for part in range(len(groups)):
                back.append(relayout(swap(sent[part][:, :, low:high])))
            back = jnp.concatenate(back, axis=1)
            kept_rows = [value[low:high] for value in states[block]]
            cuts = [0, high - low]
            if fast and block == last and sub == len(subs) - 1 and high - low > 1:
                cuts = [0, (high - low) // 2, high - low]
            blocks = [[] for _ in cuts[1:]]
            for shift in range(1, chan):
                leaving = points(back, shift, kept_rows[shift])
                for part in range(len(cuts) - 1):
                    blocks[part].append(ring(leaving[cuts[part] : cuts[part + 1]], shift))
            kept = points(back, 0, kept_rows[0])
            if not fast:
                continue
            for part in range(len(cuts) - 1):
                at = cuts[part]
                out = mlp_rows(
                    chan,
                    here,
                    [kept] + blocks[part],
                    mask_columns,
                    ring_inner,
                    ring_outer,
                    out,
                    row + low + at,
                    cuts[part + 1] - at,
                    at,
                )
        if fast:
            continue
        blocks = [kept] + blocks[0]
        ocean_mask = land_mask[row : row + row_step].astype(F32)
        full = jnp.take(jnp.stack(blocks, axis=2), (here - jnp.arange(chan)) % chan, axis=2)
        full = full.reshape(row_step, piece, chan * channels)
        pre_act = jnp.einsum("rpc,ch->rph", full, inner_full, preferred_element_type=F32)
        activated = jax.nn.gelu(pre_act).astype(BF16)
        update = jnp.einsum("rph,hc->rpc", activated, outer_full, preferred_element_type=F32)
        outs.append((ocean_mask[:, :, None] * (full.astype(F32) + update)).astype(BF16))
    return jnp.concatenate(outs, axis=0) if outs else out


def solution(mesh):
    placed = (
        P("lat", "chan", None),
        P("lat", "chan"),
        P(),
        P("lat", None, "chan", None),
        P(None, "chan"),
        P("chan", None),
    )
    lat, chan = mesh.shape["lat"], mesh.shape["chan"]

    def body(*args):
        return local(lat, chan, *args)

    return jax.shard_map(
        body, mesh=mesh, in_specs=placed, out_specs=P("lat", "chan", None), check_vma=False
    )
```

```python
import math

import jax
import jax.numpy as jnp
from jax import lax
from jax.experimental import pallas as pl
from jax.experimental.pallas import tpu as pltpu
from jax.sharding import PartitionSpec as P

BF16 = jnp.bfloat16
F32 = jnp.float32
STEP_BITS = 64.0
BIG = 2.0**64
SMALL = 2.0**-64


def turn_pair(count, period):
    count = count.astype(F32)
    count = count - jnp.floor(count * (1.0 / period)) * period
    quarter = jnp.floor(count * (4.0 / period) + 0.5)
    angle = (4.0 * count - quarter * period) * (math.pi / (2.0 * period))
    square = angle * angle
    cosine, sine = 1.0 / math.factorial(10), 1.0 / math.factorial(11)
    for k in (4, 3, 2, 1, 0):
        cosine = 1.0 / math.factorial(2 * k) - square * cosine
        sine = 1.0 / math.factorial(2 * k + 1) - square * sine
    sine = sine * angle
    quarter = quarter - 4.0 * jnp.floor(quarter * 0.25)
    odd = (quarter == 1.0) | (quarter == 3.0)
    first, second = jnp.where(odd, sine, cosine), jnp.where(odd, cosine, sine)
    first = jnp.where((quarter == 1.0) | (quarter == 2.0), -first, first)
    return first, jnp.where(quarter >= 2.0, -second, second)


def fejer_weights(row_index, nlat):
    harmonic = jnp.arange(1, nlat // 2 + 1, dtype=jnp.int32)
    cosine, _ = turn_pair(harmonic[:, None] * (2 * row_index + 1)[None, :], 2 * nlat)
    harmonic = harmonic.astype(F32)
    series = cosine / (4.0 * harmonic * harmonic - 1.0)[:, None]
    return 2.0 / nlat * (1.0 - 2.0 * jnp.sum(series, axis=0))


def legendre_kernel(upper_ref, lower_ref, mant_ref, expo_ref, cos_ref, quad_ref, weighted_ref, *rest):
    plain_refs, rows_ref = rest[:-1], rest[-1]
    width = plain_refs[0].shape[2]
    slots, modes = upper_ref.shape
    nlat = cos_ref.shape[1]
    groups = range(slots // 8)

    def scales(expo):
        one = jnp.ones_like(expo)
        first = jnp.where(expo < -0.5, one * SMALL, one)
        second = jnp.where(expo < -1.5, one * SMALL, one)
        return first, jnp.where(expo < -2.5, 0.0 * one, second)

    @pl.when(pl.program_id(0) == 0)
    def _():
        cosine = jnp.broadcast_to(cos_ref[...], (8, nlat))

        def eight(lane, carry):
            states, coefs = carry
            base = lane * (8 * slots)
            states = list(states)
            for j in range(8):
                for g in groups:
                    before, last, expo, first, second = states[g]
                    upper, lower = coefs[g]
                    a = jnp.broadcast_to(upper[:, j : j + 1], (8, nlat))
                    b = jnp.broadcast_to(lower[:, j : j + 1], (8, nlat))
                    fresh = (a * cosine) * last - b * before
                    states[g] = (last, fresh, expo, first, second)
                    value = (fresh * first) * second
                    at = pl.multiple_of(base + j * slots + 8 * g, 8)
                    for c in range(nlat // 128):
                        rows_ref[c, pl.ds(at, 8), :] = value[:, c * 128 : c * 128 + 128]
            for g in groups:
                before, last, expo, first, second = states[g]
                large = jnp.abs(last) > BIG
                before = jnp.where(large, before * SMALL, before)
                last = jnp.where(large, last * SMALL, last)
                expo = jnp.where(large, expo + 1.0, expo)
                states[g] = (before, last, expo) + scales(expo)
            coefs = tuple((pltpu.roll(u, 120, 1), pltpu.roll(w, 120, 1)) for u, w in coefs)
            return tuple(states), coefs

        states = []
        for g in groups:
            expo = expo_ref[8 * g : 8 * g + 8, :]
            mant = mant_ref[8 * g : 8 * g + 8, :]
            states.append((-mant, jnp.zeros((8, nlat), F32), expo) + scales(expo))
        states = tuple(states)

        def lane_block(block, states):
            lanes = pl.ds(pl.multiple_of(block * 128, 128), 128)
            coefs = tuple(
                (upper_ref[8 * g : 8 * g + 8, lanes], lower_ref[8 * g : 8 * g + 8, lanes]) for g in groups
            )
            body = lambda turn, carry: eight(block * 16 + turn, carry)
            return lax.fori_loop(0, 16, body, (states, coefs))[0]

        lax.fori_loop(0, modes // 128, lane_block, states)

    for c in range(nlat // 128):
        lanes = slice(c * 128, c * 128 + 128)
        quad = quad_ref[:, lanes]
        plain_ref, at = plain_refs[c * 128 // width], c * 128 % width

        @pl.loop(0, 8)
        def _(k):
            values = rows_ref[c, pl.ds(pl.program_id(0) * 8 + k, modes, stride=slots), :]
            plain_ref[k, :, at : at + 128] = values.astype(BF16)
            weighted_ref[k, :, lanes] = (values * quad).astype(BF16)


def row_order(lat, rows, row_step):
    row = jnp.arange(lat * rows, dtype=jnp.int32)
    block, owner, inner = row // (lat * row_step), row // row_step % lat, row % row_step
    return owner * rows + block * row_step + inner


def legendre_tables(orders, row_index, quad, nlat, modes, width):
    slots = orders.shape[0]
    padded = -(-slots // 8) * 8
    orders = jnp.pad(orders, (0, padded - slots))
    half_sign = jnp.where(row_index < nlat // 2, 1.0, -1.0).astype(F32)
    north = jnp.minimum(row_index, nlat - 1 - row_index)
    cosine, sine = turn_pair(2 * north + 1, 4 * nlat)
    cosine = cosine * half_sign
    order = orders.astype(F32)[:, None]
    offset = jnp.arange(modes).astype(F32)[None, :]
    degree = order + offset
    inside = (offset >= 1.0) & (offset < modes - order)
    upper = jnp.sqrt(
        (4.0 * degree * degree - 1.0)
        / jnp.where(offset >= 1.0, offset * (degree + order), 1.0)
    )
    previous = degree - 1.0
    lower = jnp.sqrt(
        jnp.maximum((offset - 1.0) * (previous + order), 0.0)
        / jnp.maximum(4.0 * previous * previous - 1.0, 1.0)
    )
    upper_coef = jnp.where(inside, upper, 0.0)
    lower_coef = jnp.where(inside, upper * lower, jnp.where(offset < 0.5, 1.0, 0.0))
    steps_log = 0.5 * jnp.log((2.0 * offset + 3.0) / (2.0 * offset + 2.0))
    picked = jnp.sum(jnp.where(offset < order, steps_log, 0.0), axis=1, keepdims=True)
    start_log = 0.5 * math.log(0.5) + picked + order * jnp.log(sine)[None, :]
    unit = STEP_BITS * math.log(2.0)
    expo = jnp.floor(start_log / unit)
    mant = jnp.exp(start_log - expo * unit)
    each = lambda wide: pl.BlockSpec((padded, wide), lambda g: (0, 0))
    whole = lambda wide: pl.BlockSpec((1, wide), lambda g: (0, 0))
    table = lambda wide: pl.BlockSpec((8, modes, wide), lambda g: (g, 0, 0))
    shape = lambda wide: jax.ShapeDtypeStruct((padded, modes, wide), BF16)
    blocks = nlat // width
    weighted, *plain = pl.pallas_call(
        legendre_kernel,
        grid=(padded // 8,),
        in_specs=[each(modes), each(modes), each(nlat), each(nlat), whole(nlat), whole(nlat)],
        out_specs=[table(nlat)] + [table(width)] * blocks,
        out_shape=[shape(nlat)] + [shape(width)] * blocks,
        scratch_shapes=[pltpu.VMEM((nlat // 128, modes * padded, 128), F32)],
        cost_estimate=pl.CostEstimate(
            flops=padded * modes * nlat * 16, bytes_accessed=padded * modes * nlat * 4, transcendentals=0
        ),
        name="legendre",
    )(upper_coef, lower_coef, mant, expo, cosine[None, :], quad[None, :])
    return weighted[:slots], [table[:slots] for table in plain]


def fourier_columns(orders, nlon):
    inner = 8 if nlon % 8 == 0 else 1
    slots = orders.shape[0]
    column_order = jnp.repeat(orders, 2)
    part = jnp.tile(jnp.arange(2, dtype=jnp.int32), slots)

    def pair(steps, shifted):
        cosine, sine = turn_pair(column_order[None, :] * steps[:, None], nlon)
        if not shifted:
            return cosine, sine
        odd = (part == 1)[None, :]
        return jnp.where(odd, -sine, cosine), jnp.where(odd, cosine, sine)

    far_cos, far_sin = pair(jnp.arange(nlon // inner, dtype=jnp.int32) * inner, True)
    near_cos, near_sin = pair(jnp.arange(inner, dtype=jnp.int32), False)
    value = far_cos[:, None, :] * near_cos[None] - far_sin[:, None, :] * near_sin[None]
    value = value.reshape(nlon, 2 * slots)
    factor = jnp.where(column_order == 0, 1.0, 2.0).astype(F32) / math.sqrt(2.0 * math.pi)
    forward = (value * (math.sqrt(2.0 * math.pi) / nlon)).astype(BF16)
    inverse = (value * factor[None, :]).astype(BF16)
    return forward, inverse


def mixing_blocks(weights):
    real_part = weights[:, 0]
    imag_part = weights[:, 1]
    return jnp.stack(
        [jnp.stack([real_part, imag_part], axis=1), jnp.stack([-imag_part, real_part], axis=1)],
        axis=1,
    )


def mlp_kernel(chan, first_row, here_ref, mask_ref, inner_ref, outer_ref, *rest):
    block_refs, out_ref = rest[:chan], rest[-1]
    channels = block_refs[0].shape[2]
    row = pl.program_id(0) + first_row
    lane = lax.broadcasted_iota(jnp.int32, mask_ref.shape, 1)
    mask = jnp.sum(jnp.where(lane == row, mask_ref[...], 0.0), axis=1, keepdims=True)
    points = jnp.concatenate([ref[0] for ref in block_refs], axis=1)
    pre_act = jnp.dot(points, inner_ref[...], preferred_element_type=F32)
    activated = jax.nn.gelu(pre_act).astype(BF16)
    update = jnp.dot(activated, outer_ref[...], preferred_element_type=F32)
    for shift, block_ref in enumerate(block_refs):
        start = pl.multiple_of(lax.rem(here_ref[0] - shift + chan, chan) * channels, channels)
        lanes = slice(shift * channels, (shift + 1) * channels)
        total = mask * (block_ref[0].astype(F32) + update[:, lanes])
        out_ref[0, :, pl.ds(start, channels)] = total.astype(BF16)


def mlp_rows(chan, here, blocks, mask, inner, outer, filled, row, row_step, kept_at):
    rows = mask.shape[1]
    _, piece, channels = blocks[0].shape
    whole = lambda shape: pl.BlockSpec(shape, lambda r, h: (0, 0))
    in_specs = [whole((piece, rows)), whole(inner.shape), whole(outer.shape)]
    in_specs += [pl.BlockSpec((1, piece, channels), lambda r, h: (r + kept_at, 0, 0))]
    in_specs += [pl.BlockSpec((1, piece, channels), lambda r, h: (r, 0, 0))] * (chan - 1)
    operands = [here.reshape(1), mask, inner, outer] + blocks
    aliases = {}
    if filled is not None:
        aliases = {len(operands): 0}
        operands.append(filled)
        in_specs.append(pl.BlockSpec(memory_space=pl.ANY))
    width = chan * channels
    return pl.pallas_call(
        lambda *refs: mlp_kernel(chan, row, *refs),
        grid_spec=pltpu.PrefetchScalarGridSpec(
            num_scalar_prefetch=1,
            grid=(row_step,),
            in_specs=in_specs,
            out_specs=pl.BlockSpec((1, piece, width), lambda r, h: (r + row, 0, 0)),
        ),
        out_shape=jax.ShapeDtypeStruct((rows, piece, width), BF16),
        input_output_aliases=aliases,
        cost_estimate=pl.CostEstimate(
            flops=4 * row_step * piece * width * inner.shape[1],
            bytes_accessed=4 * row_step * piece * width,
            transcendentals=row_step * piece * inner.shape[1],
        ),
        name="pointwise",
    )(*operands)


def local(lat, chan, ocean_state, land_mask, order_table, spectral_weight, inner_weight, outer_weight):
    rows, channels, nlon = ocean_state.shape
    slots = spectral_weight.shape[0]
    modes = order_table.shape[0]
    nlat = rows * lat
    piece = nlon // chan
    slot_step = 8 if slots % 8 == 0 else slots
    row_step = 8 if rows % 8 == 0 and lat * 8 % 128 == 0 else rows
    width = lat * row_step
    here = lax.axis_index("chan")

    def ring(value, shift):
        return lax.ppermute(value, "chan", [(i, (i + shift) % chan) for i in range(chan)])

    def swap(value):
        return lax.all_to_all(value, "lat", split_axis=0, concat_axis=0, tiled=True)

    inner_parts = [inner_weight] + [ring(inner_weight, shift) for shift in range(1, chan)]
    outer_parts = [outer_weight] + [ring(outer_weight, shift) for shift in range(1, chan)]
    inner_full = jnp.concatenate(inner_parts, axis=1)
    outer_full = jnp.concatenate(outer_parts, axis=0)
    pieces = [(here + shift) % chan for shift in range(chan)]
    sources = [(here - shift) % chan for shift in range(chan)]
    take = lambda value, at, size, axis: lax.dynamic_slice_in_dim(value, at * size, size, axis=axis)
    order_of = [[(at - shift) % chan for shift in range(chan)] for at in range(chan)]
    arranged = lambda value, axis, at: jnp.concatenate(
        [jnp.split(value, chan, axis=axis)[block] for block in order_of[at]], axis=axis
    )
    ring_inner, ring_outer = arranged(inner_full, 0, 0), arranged(outer_full, 1, 0)
    for at in range(1, chan):
        ring_inner = jnp.where(here == at, arranged(inner_full, 0, at), ring_inner)
        ring_outer = jnp.where(here == at, arranged(outer_full, 1, at), ring_outer)
    ring_inner, ring_outer = lax.optimization_barrier((ring_inner, ring_outer))
    my_orders = lax.dynamic_slice_in_dim(order_table, lax.axis_index("lat") * slots, slots)
    by_owner = order_table.reshape(lat, slots)
    starts = range(0, slots, slot_step)
    received, inverses = [], []
    for start in starts:
        orders = by_owner[:, start : start + slot_step].reshape(-1)
        forward, inverse = lax.optimization_barrier(fourier_columns(orders, nlon))
        inverses.append(inverse)
        coeffs = lax.dot_general(
            forward, ocean_state, (((0,), (2,)), ((), ())), preferred_element_type=F32
        ).astype(BF16)
        received.append(swap(coeffs))
    mixers = lax.optimization_barrier(
        [
            [
                mixing_blocks(take(spectral_weight[start : start + slot_step], at, channels, 3))
                for at in sources
            ]
            for start in starts
        ]
    )
    row_index = row_order(lat, rows, row_step)
    quad = fejer_weights(row_index, nlat)
    tables = {}
    spans = [(0, slot_step), (slot_step, slots)] if slots > slot_step else [(0, slots)]
    for first, end in spans:
        weighted_all, plain_all = legendre_tables(
            my_orders[first:end], row_index, quad, nlat, modes, width
        )
        for start in range(first, end, slot_step):
            part = slice(start - first, start - first + slot_step)
            tables[start] = (weighted_all[part], [table[part] for table in plain_all])
    mixed, plains = [], []
    for index, (coeffs, start) in enumerate(zip(received, starts)):
        weighted, plain = tables[start]
        plains.append(plain)
        coeffs = coeffs.reshape(lat, slot_step, 2, rows // row_step, row_step, channels)
        coeffs = jnp.transpose(coeffs, (1, 2, 3, 0, 4, 5)).reshape(slot_step, 2, nlat, channels)
        spectra = jnp.einsum(
            "sprc,sir->spic", coeffs, weighted, preferred_element_type=F32
        ).astype(BF16)
        total = None
        for shift in range(chan):
            arrived = spectra if shift == 0 else ring(spectra, shift)
            term = jnp.einsum("spic,spqdc->sqid", arrived, mixers[index][shift], preferred_element_type=F32)
            if shift == 0 and chan > 1:
                term = lax.optimization_barrier(term)
            total = term if total is None else total + term
        mixed.append(total.astype(BF16))
    inverse = jnp.concatenate(inverses, axis=1)
    inverse_of = lax.optimization_barrier(
        [lax.dynamic_slice_in_dim(inverse, at * piece, piece) for at in pieces]
    )
    fast = channels % 128 == 0 and piece % 8 == 0 and row_step % 8 == 0 and len(starts) > 1
    state = jnp.transpose(ocean_state.reshape(rows, channels, chan, piece), (2, 0, 3, 1))
    state = [lax.dynamic_index_in_dim(state, at, 0, keepdims=False) for at in pieces]
    states = lax.optimization_barrier(
        [[value[row : row + row_step] for value in state] for row in range(0, rows, row_step)]
    )
    mask_columns = lax.optimization_barrier(land_mask.astype(F32).T)
    out, outs = None, []
    count = len(starts)

    def relayout(arrived):
        return jnp.transpose(arrived, (2, 1, 0, 3, 4, 5)).reshape(arrived.shape[2], -1, channels)

    def points(back, at, state):
        spatial = jnp.einsum("rkd,jk->rjd", back, inverse_of[at], preferred_element_type=F32)
        return (state.astype(F32) + spatial).astype(BF16)

    last = rows // row_step - 1
    for block, row in enumerate(range(0, rows, row_step)):
        groups = [list(range(count))]
        if fast and block == 0:
            groups = [list(range(count - 1)), [count - 1]]
        subs = [(0, row_step)]
        if fast and block == last and block > 0:
            subs = [(0, row_step // 2), (row_step // 2, row_step)]
        sent = []
        for part, group in enumerate(groups):
            made = [
                jnp.einsum("sqid,sir->rsqd", mixed[g], plains[g][block], preferred_element_type=F32)
                .astype(BF16)
                .reshape(lat, row_step, slot_step, 2, channels)
                for g in group
            ]
            sent.append(jnp.stack(made, axis=1))
        for sub, (low, high) in enumerate(subs):
            back = []
            for part in range(len(groups)):
                back.append(relayout(swap(sent[part][:, :, low:high])))
            back = jnp.concatenate(back, axis=1)
            kept_rows = [value[low:high] for value in states[block]]
            cuts = [0, high - low]
            if fast and block == last and sub == len(subs) - 1 and high - low > 1:
                cuts = [0, (high - low) // 2, high - low]
            blocks = [[] for _ in cuts[1:]]
            for shift in range(1, chan):
                leaving = points(back, shift, kept_rows[shift])
                for part in range(len(cuts) - 1):
                    blocks[part].append(ring(leaving[cuts[part] : cuts[part + 1]], shift))
            kept = points(back, 0, kept_rows[0])
            if not fast:
                continue
            for part in range(len(cuts) - 1):
                at = cuts[part]
                out = mlp_rows(
                    chan,
                    here,
                    [kept] + blocks[part],
                    mask_columns,
                    ring_inner,
                    ring_outer,
                    out,
                    row + low + at,
                    cuts[part + 1] - at,
                    at,
                )
        if fast:
            continue
        blocks = [kept] + blocks[0]
        ocean_mask = land_mask[row : row + row_step].astype(F32)
        full = jnp.take(jnp.stack(blocks, axis=2), (here - jnp.arange(chan)) % chan, axis=2)
        full = full.reshape(row_step, piece, chan * channels)
        pre_act = jnp.einsum("rpc,ch->rph", full, inner_full, preferred_element_type=F32)
        activated = jax.nn.gelu(pre_act).astype(BF16)
        update = jnp.einsum("rph,hc->rpc", activated, outer_full, preferred_element_type=F32)
        outs.append((ocean_mask[:, :, None] * (full.astype(F32) + update)).astype(BF16))
    return jnp.concatenate(outs, axis=0) if outs else out


def solution(mesh):
    placed = (
        P("lat", "chan", None),
        P("lat", "chan"),
        P(),
        P("lat", None, "chan", None),
        P(None, "chan"),
        P("chan", None),
    )
    lat, chan = mesh.shape["lat"], mesh.shape["chan"]

    def body(*args):
        return local(lat, chan, *args)

    return jax.shard_map(
        body, mesh=mesh, in_specs=placed, out_specs=P("lat", "chan", None), check_vma=False
    )
```
